512 devices in a mesh: seq: 64 (over x, z_hi, y), sub: 8 (over z_lo, core).
Axes of the slice: x: 4, y: 4, z: 16 (z_hi: 4, z_lo: 4; z = z_hi * 4 + z_lo), core: 2. Of those that a mesh axis runs over, the one named last changes fastest.
Arguments:
- activation: bfloat16 [65536, 1024], P(('sub', 'seq')), may hold values from -6 to 6
- filter_raw: bfloat16 [65536, 1024], P(('sub', 'seq')), may hold values from -6 to 6
- decay_rate: float32 [1024], replicated, may hold values from 0.5 to 16
- skip_gain: float32 [1024], replicated, may hold values from 0.5 to 2
- grad_out: bfloat16 [65536, 1024], P(('sub', 'seq')), may hold values from -6 to 6
Outputs:
- grad_input: bfloat16 [65536, 1024], P(('sub', 'seq'))
- grad_raw: bfloat16 [65536, 1024], P(('sub', 'seq'))
The draws below stay inside these ranges and needn't reach their ends.
All inputs are finite; a program needn't handle non-finite values.
Results may differ from the reference program's by a relative error of at most 0.001.
Values may be sent and summed in bfloat16 or wider, within the bound.
A program may use at most 64 MiB of HBM per device.

```python
import math
import jax
import jax.numpy as jnp
from jax import lax

D = 1024
TOKENS = 65536


def block_scale(key, shape, shards, smallest, top_value):
    def one(dim, blocks):
        draws = jax.random.uniform(jax.random.fold_in(jax.random.fold_in(key, 6), dim), (blocks,), jnp.float32, smallest / len(shards), top_value / len(shards))
        return jnp.repeat(jnp.exp(draws), shape[dim] // blocks).reshape((-1,) + (1,) * (len(shape) - dim - 1))

    factor_of = one(*shards[0])
    for cut in shards[1:]:
        factor_of = factor_of * one(*cut)
    return factor_of


def normal_values(own_key, dims, deviation, bound, split=(), held_as=jnp.bfloat16):
    factor_of = block_scale(own_key, dims, split, -0.22, 0.18) if split else 1.0
    values = jax.random.normal(own_key, dims, jnp.float32) * deviation * factor_of
    return jnp.minimum(jnp.maximum(values, -bound), bound).astype(held_as)


def setup_inputs(seed: int = 0) -> dict:
    streams_of = jax.random.split(jax.random.key(seed), 6)
    return {
        "activation": normal_values(streams_of[0], (TOKENS, D), 1.0, 6.0, ((0, 512),)),
        "filter_raw": normal_values(streams_of[1], (TOKENS, D), 1.0, 6.0, ((0, 512),)),
        "decay_rate": jnp.clip(jnp.exp(jax.random.uniform(streams_of[2], (D,), jnp.float32, math.log(0.5), math.log(16.0))), 0.5, 16.0),
        "skip_gain": jnp.clip(jnp.exp(jax.random.uniform(streams_of[3], (D,), jnp.float32, math.log(0.5), math.log(2.0))), 0.5, 2.0),
        "grad_out": normal_values(streams_of[4], (TOKENS, D), 1.0, 6.0, ((0, 512),)),
    }


lane_block = 64

def split_lanes(values):
    return jnp.transpose(values.reshape(TOKENS, D // lane_block, lane_block), (1, 0, 2))

def join_lanes(values):
    return jnp.transpose(values, (1, 0, 2)).reshape(TOKENS, D)

def correlations(lanes):
    source, filter_taps, upstream = lanes
    length = 2 * TOKENS
    spec_up = jnp.fft.rfft(upstream, n=length, axis=0)
    spec_taps = jnp.fft.rfft(filter_taps, n=length, axis=0)
    spec_source = jnp.fft.rfft(source, n=length, axis=0)
    through = jnp.fft.irfft(spec_up * jnp.conj(spec_taps), n=length, axis=0)[:TOKENS]
    across = jnp.fft.irfft(spec_up * jnp.conj(spec_source), n=length, axis=0)[:TOKENS]
    return (through.astype(jnp.float32), across.astype(jnp.float32))

def reference(activation, filter_raw, decay_rate, skip_gain, grad_out):
    positions = jnp.arange(TOKENS, dtype=jnp.float32)[:, None]
    envelope = jnp.sqrt(2.0 * decay_rate / TOKENS)[None, :] * jnp.exp(-(decay_rate[None, :] * positions) / TOKENS)
    filter_taps = filter_raw.astype(jnp.float32) * envelope
    act_float = activation.astype(jnp.float32)
    up_float = grad_out.astype(jnp.float32)
    conv_grad, filt_grad = lax.map(correlations, (split_lanes(act_float), split_lanes(filter_taps), split_lanes(up_float)))
    conv_grad = join_lanes(conv_grad)
    filt_grad = join_lanes(filt_grad)
    grad_input = (conv_grad + skip_gain[None, :] * up_float).astype(jnp.bfloat16)
    grad_raw = (filt_grad * envelope).astype(jnp.bfloat16)
    return (grad_input, grad_raw)
```

```python
import functools
import math

import jax
import jax.numpy as jnp
from jax import lax
from jax.experimental import pallas as pl
from jax.experimental.pallas import tpu as pltpu
from jax.sharding import PartitionSpec as P

both = ("sub", "seq")
two_stage = True


def split_halves(values):
    high = lax.reduce_precision(values, 8, 7)
    return high.astype(jnp.bfloat16), (values - high).astype(jnp.bfloat16)


def halves(values):
    high = values.astype(jnp.bfloat16)
    return high, (values - high.astype(jnp.float32)).astype(jnp.bfloat16)


def mul(left, right):
    return jnp.dot(left, right, preferred_element_type=jnp.float32)


def mul3(left, right):
    left_hi, left_lo = left
    right_hi, right_lo = right
    return mul(left_hi, right_hi) + (mul(left_hi, right_lo) + mul(left_lo, right_hi))


def correlate(
    chan, cell, chunk, scale,
    got_ref, env_ref, gain_ref, fwd_hi_ref, fwd_lo_ref, back_hi_ref, back_lo_ref,
    inner_hi_ref, inner_lo_ref, outer_hi_ref, outer_lo_ref, cos_ref, sin_ref,
    out_ref, taps_hi_ref, taps_lo_ref, total_ref,
):
    step = pl.program_id(0)
    width = chan * cell

    @pl.when(step == 0)
    def _():
        taps = got_ref[:, width : 2 * width].astype(jnp.float32) * env_ref[...]
        high, low = halves(taps)
        taps_hi_ref[...] = high
        taps_lo_ref[...] = low
        total_ref[...] = jnp.zeros_like(total_ref)

    fwd_hi = fwd_hi_ref[...]
    fwd_lo = fwd_lo_ref[...]
    act = got_ref[:, 0:width]
    up = got_ref[:, 2 * width : 3 * width]
    first = (
        mul(fwd_hi, act) + mul(fwd_lo, act),
        mul(fwd_hi, taps_hi_ref[...])
        + (mul(fwd_hi, taps_lo_ref[...]) + mul(fwd_lo, taps_hi_ref[...])),
        mul(fwd_hi, up) + mul(fwd_lo, up),
    )
    cosine = cos_ref[...]
    sine = sin_ref[...]
    inner = (inner_hi_ref[...], inner_lo_ref[...])
    outer = (outer_hi_ref[...], outer_lo_ref[...])
    spectra = []
    for values in first:
        rows = []
        for c in range(chan):
            re = values[:chunk, c * cell : (c + 1) * cell]
            im = values[chunk:, c * cell : (c + 1) * cell]
            rows.append(
                jnp.concatenate([re * cosine + im * sine, im * cosine - re * sine], axis=1)
            )
        spectra.append(mul3(halves(jnp.concatenate(rows, axis=0)), inner))
    up_re, up_im = spectra[2][:, :cell], spectra[2][:, cell:]
    parts_re, parts_im = [], []
    for other in (spectra[1], spectra[0]):
        re, im = other[:, :cell], other[:, cell:]
        mixed = jnp.concatenate([up_re * re + up_im * im, up_im * re - up_re * im], axis=1)
        back = mul3(halves(mixed), outer)
        for c in range(chan):
            zre = back[c * chunk : (c + 1) * chunk, :cell]
            zim = back[c * chunk : (c + 1) * chunk, cell:]
            parts_re.append(zre * cosine - zim * sine)
            parts_im.append(zim * cosine + zre * sine)
    spread = jnp.concatenate(
        [jnp.concatenate(parts_re, axis=1), jnp.concatenate(parts_im, axis=1)], axis=0
    )
    total_ref[...] += mul3((back_hi_ref[...], back_lo_ref[...]), halves(spread))

    @pl.when(step == pl.num_programs(0) - 1)
    def _():
        through = total_ref[:, :width] * scale
        across = total_ref[:, width:] * scale
        up_float = got_ref[:, 2 * width : 3 * width].astype(jnp.float32)
        out_ref[:, :width] = (through + gain_ref[...] * up_float).astype(jnp.bfloat16)
        out_ref[:, width:] = (across * env_ref[...]).astype(jnp.bfloat16)


def local_part(got, rate, gain, places, chan, cell, total_tokens, interpret=False):
    blocks = got.shape[0]
    chunk = min(128, blocks)
    steps = blocks // chunk
    length = 2 * total_tokens
    width = chan * cell
    freq = jnp.arange(blocks, dtype=jnp.int32)
    odd = 2 * freq + 1

    def angle(numerator, modulus):
        return (2.0 * math.pi / modulus) * (numerator % modulus).astype(jnp.float32)

    fwd_angle = angle(odd[:, None] * places[None, :], 4 * blocks).reshape(steps, 1, chunk, blocks)
    fwd = jnp.concatenate([jnp.cos(fwd_angle), -jnp.sin(fwd_angle)], 1)
    fwd_hi, fwd_lo = split_halves(fwd.reshape(2 * blocks, blocks))
    back_angle = angle(places[:, None] * odd[None, :], 4 * blocks).reshape(blocks, steps, 1, chunk)
    back = jnp.concatenate([jnp.cos(back_angle), -jnp.sin(back_angle)], 2)
    back_hi, back_lo = split_halves(back.reshape(blocks, 2 * blocks))
    cells = jnp.arange(cell, dtype=jnp.int32)
    inner_angle = angle(cells[:, None] * cells[None, :], cell)
    icos, isin = jnp.cos(inner_angle), jnp.sin(inner_angle)
    inner = jnp.concatenate(
        [jnp.concatenate([icos, -isin], 1), jnp.concatenate([isin, icos], 1)], 0
    )
    outer = jnp.concatenate(
        [jnp.concatenate([icos, isin], 1), jnp.concatenate([-isin, icos], 1)], 0
    )
    inner_hi, inner_lo = split_halves(inner)
    outer_hi, outer_lo = split_halves(outer)
    turn = angle(odd[:, None] * cells[None, :], 2 * length)
    at = (places[:, None] * cell + cells[None, :]).astype(jnp.float32)
    env = jnp.concatenate(
        [
            jnp.sqrt(2.0 * rate[c] / total_tokens) * jnp.exp(-(rate[c] * at) / total_tokens)
            for c in range(chan)
        ],
        1,
    )
    gain_row = jnp.repeat(gain, cell)[None, :]
    whole = lambda shape: pl.BlockSpec(shape, lambda i: (0, 0))
    flops = 2 * 3 * (5 * 2 * blocks * blocks * width + 5 * chan * blocks * 4 * cell * cell)
    return pl.pallas_call(
        functools.partial(correlate, chan, cell, chunk, 2.0 / length),
        grid=(steps,),
        out_shape=jax.ShapeDtypeStruct((blocks, 2 * width), jnp.bfloat16),
        in_specs=[
            whole((blocks, 3 * width)),
            whole((blocks, width)),
            whole((1, width)),
            pl.BlockSpec((2 * chunk, blocks), lambda i: (i, 0)),
            pl.BlockSpec((2 * chunk, blocks), lambda i: (i, 0)),
            pl.BlockSpec((blocks, 2 * chunk), lambda i: (0, i)),
            pl.BlockSpec((blocks, 2 * chunk), lambda i: (0, i)),
            whole((2 * cell, 2 * cell)),
            whole((2 * cell, 2 * cell)),
            whole((2 * cell, 2 * cell)),
            whole((2 * cell, 2 * cell)),
            pl.BlockSpec((chunk, cell), lambda i: (i, 0)),
            pl.BlockSpec((chunk, cell), lambda i: (i, 0)),
        ],
        out_specs=whole((blocks, 2 * width)),
        scratch_shapes=[
            pltpu.VMEM((blocks, width), jnp.bfloat16),
            pltpu.VMEM((blocks, width), jnp.bfloat16),
            pltpu.VMEM((blocks, 2 * width), jnp.float32),
        ],
        cost_estimate=pl.CostEstimate(flops=flops, bytes_accessed=8 * 2**20, transcendentals=0),
        interpret=interpret,
    )(
        got, env, gain_row, fwd_hi, fwd_lo, back_hi, back_lo,
        inner_hi, inner_lo, outer_hi, outer_lo, jnp.cos(turn), jnp.sin(turn),
    )


def per_device(activation, filter_raw, decay_rate, skip_gain, grad_out, interpret=False):
    cell, model_width = activation.shape
    seq_count = lax.axis_size("seq")
    sub_count = lax.axis_size("sub")
    blocks = seq_count * sub_count
    chan = model_width // blocks
    seq_at = lax.axis_index("seq")
    sub_at = lax.axis_index("sub")
    leaving = jnp.stack(
        [jnp.transpose(v).reshape(blocks, chan, cell) for v in (activation, filter_raw, grad_out)],
        axis=1,
    )
    row = jnp.arange(blocks, dtype=jnp.int32)
    if two_stage:
        leaving = leaving.reshape(sub_count, seq_count, 3, chan, cell)
        near = lax.all_to_all(leaving, "sub", 0, 0)
        near = jnp.transpose(near, (1, 0, 2, 3, 4))
        got = lax.all_to_all(near, "seq", 0, 0).reshape(blocks, 3 * chan * cell)
        places = (row % sub_count) * seq_count + row // sub_count
    else:
        got = lax.all_to_all(leaving, both, 0, 0).reshape(blocks, 3 * chan * cell)
        places = row
    first_chan = (sub_at * seq_count + seq_at) * chan
    rate = lax.dynamic_slice_in_dim(decay_rate, first_chan, chan)
    gain = lax.dynamic_slice_in_dim(skip_gain, first_chan, chan)
    done = local_part(got, rate, gain, places, chan, cell, blocks * cell, interpret)
    if two_stage:
        done = done.reshape(seq_count, sub_count, 2, chan, cell)
        far = jnp.transpose(lax.all_to_all(done, "seq", 0, 0), (1, 0, 2, 3, 4))
        back = lax.all_to_all(far, "sub", 0, 0)
    else:
        back = lax.all_to_all(done.reshape(blocks, 2, chan, cell), both, 0, 0)
    back = back.reshape(blocks, 2, chan, cell)
    return tuple(
        jnp.transpose(back[:, o].reshape(model_width, cell)) for o in range(2)
    )


def solution(mesh, interpret=False):
    return jax.shard_map(
        functools.partial(per_device, interpret=interpret),
        mesh=mesh,
        in_specs=(P(both, None), P(both, None), P(), P(), P(both, None)),
        out_specs=(P(both, None), P(both, None)),
        check_vma=False,
    )
```

```python
import functools
import math

import jax
import jax.numpy as jnp
from jax import lax
from jax.experimental import pallas as pl
from jax.experimental.pallas import tpu as pltpu
from jax.sharding import PartitionSpec as P

tokens_over = ("zl", "core", "x", "zh", "y")
plane = ("x", "y", "core")
ring = ("zh", "zl")


def split_halves(values):
    high = lax.reduce_precision(values, 8, 7)
    return high.astype(jnp.bfloat16), (values - high).astype(jnp.bfloat16)


def halves(values):
    high = values.astype(jnp.bfloat16)
    return high, (values - high.astype(jnp.float32)).astype(jnp.bfloat16)


def mul(left, right):
    return jnp.dot(left, right, preferred_element_type=jnp.float32)


def mul3(left, right):
    left_hi, left_lo = left
    right_hi, right_lo = right
    return mul(left_hi, right_hi) + (mul(left_hi, right_lo) + mul(left_lo, right_hi))


def correlate(
    chan, cell, chunk, scale,
    got_ref, env_ref, gain_ref, fwd_hi_ref, fwd_lo_ref, back_hi_ref, back_lo_ref,
    inner_hi_ref, inner_lo_ref, outer_hi_ref, outer_lo_ref, cos_ref, sin_ref,
    out_ref, taps_hi_ref, taps_lo_ref, total_ref,
):
    step = pl.program_id(0)
    width = chan * cell

    @pl.when(step == 0)
    def _():
        taps = got_ref[:, width : 2 * width].astype(jnp.float32) * env_ref[...]
        high, low = halves(taps)
        taps_hi_ref[...] = high
        taps_lo_ref[...] = low
        total_ref[...] = jnp.zeros_like(total_ref)

    fwd_hi = fwd_hi_ref[...]
    fwd_lo = fwd_lo_ref[...]
    act = got_ref[:, 0:width]
    up = got_ref[:, 2 * width : 3 * width]
    first = (
        mul(fwd_hi, act) + mul(fwd_lo, act),
        mul(fwd_hi, taps_hi_ref[...])
        + (mul(fwd_hi, taps_lo_ref[...]) + mul(fwd_lo, taps_hi_ref[...])),
        mul(fwd_hi, up) + mul(fwd_lo, up),
    )
    cosine = cos_ref[...]
    sine = sin_ref[...]
    inner = (inner_hi_ref[...], inner_lo_ref[...])
    outer = (outer_hi_ref[...], outer_lo_ref[...])
    spectra = []
    for values in first:
        rows = []
        for c in range(chan):
            re = values[:chunk, c * cell : (c + 1) * cell]
            im = values[chunk:, c * cell : (c + 1) * cell]
            rows.append(
                jnp.concatenate([re * cosine + im * sine, im * cosine - re * sine], axis=1)
            )
        spectra.append(mul3(halves(jnp.concatenate(rows, axis=0)), inner))
    up_re, up_im = spectra[2][:, :cell], spectra[2][:, cell:]
    parts_re, parts_im = [], []
    for other in (spectra[1], spectra[0]):
        re, im = other[:, :cell], other[:, cell:]
        mixed = jnp.concatenate([up_re * re + up_im * im, up_im * re - up_re * im], axis=1)
        back = mul3(halves(mixed), outer)
        for c in range(chan):
            zre = back[c * chunk : (c + 1) * chunk, :cell]
            zim = back[c * chunk : (c + 1) * chunk, cell:]
            parts_re.append(zre * cosine - zim * sine)
            parts_im.append(zim * cosine + zre * sine)
    spread = jnp.concatenate(
        [jnp.concatenate(parts_re, axis=1), jnp.concatenate(parts_im, axis=1)], axis=0
    )
    total_ref[...] += mul3((back_hi_ref[...], back_lo_ref[...]), halves(spread))

    @pl.when(step == pl.num_programs(0) - 1)
    def _():
        through = total_ref[:, :width] * scale
        across = total_ref[:, width:] * scale
        up_float = got_ref[:, 2 * width : 3 * width].astype(jnp.float32)
        out_ref[:, :width] = (through + gain_ref[...] * up_float).astype(jnp.bfloat16)
        out_ref[:, width:] = (across * env_ref[...]).astype(jnp.bfloat16)


def local_part(got, rate, gain, places, chan, cell, total_tokens, interpret=False):
    blocks = got.shape[0]
    chunk = min(128, blocks)
    steps = blocks // chunk
    length = 2 * total_tokens
    width = chan * cell
    freq = jnp.arange(blocks, dtype=jnp.int32)
    odd = 2 * freq + 1

    def angle(numerator, modulus):
        return (2.0 * math.pi / modulus) * (numerator % modulus).astype(jnp.float32)

    fwd_angle = angle(odd[:, None] * places[None, :], 4 * blocks).reshape(steps, 1, chunk, blocks)
    fwd = jnp.concatenate([jnp.cos(fwd_angle), -jnp.sin(fwd_angle)], 1)
    fwd_hi, fwd_lo = split_halves(fwd.reshape(2 * blocks, blocks))
    back_angle = angle(places[:, None] * odd[None, :], 4 * blocks).reshape(blocks, steps, 1, chunk)
    back = jnp.concatenate([jnp.cos(back_angle), -jnp.sin(back_angle)], 2)
    back_hi, back_lo = split_halves(back.reshape(blocks, 2 * blocks))
    cells = jnp.arange(cell, dtype=jnp.int32)
    inner_angle = angle(cells[:, None] * cells[None, :], cell)
    icos, isin = jnp.cos(inner_angle), jnp.sin(inner_angle)
    inner = jnp.concatenate(
        [jnp.concatenate([icos, -isin], 1), jnp.concatenate([isin, icos], 1)], 0
    )
    outer = jnp.concatenate(
        [jnp.concatenate([icos, isin], 1), jnp.concatenate([-isin, icos], 1)], 0
    )
    inner_hi, inner_lo = split_halves(inner)
    outer_hi, outer_lo = split_halves(outer)
    turn = angle(odd[:, None] * cells[None, :], 2 * length)
    at = (places[:, None] * cell + cells[None, :]).astype(jnp.float32)
    env = jnp.concatenate(
        [
            jnp.sqrt(2.0 * rate[c] / total_tokens) * jnp.exp(-(rate[c] * at) / total_tokens)
            for c in range(chan)
        ],
        1,
    )
    gain_row = jnp.repeat(gain, cell)[None, :]
    whole = lambda shape: pl.BlockSpec(shape, lambda i: (0, 0))
    flops = 2 * 3 * (5 * 2 * blocks * blocks * width + 5 * chan * blocks * 4 * cell * cell)
    return pl.pallas_call(
        functools.partial(correlate, chan, cell, chunk, 2.0 / length),
        grid=(steps,),
        out_shape=jax.ShapeDtypeStruct((blocks, 2 * width), jnp.bfloat16),
        in_specs=[
            whole((blocks, 3 * width)),
            whole((blocks, width)),
            whole((1, width)),
            pl.BlockSpec((2 * chunk, blocks), lambda i: (i, 0)),
            pl.BlockSpec((2 * chunk, blocks), lambda i: (i, 0)),
            pl.BlockSpec((blocks, 2 * chunk), lambda i: (0, i)),
            pl.BlockSpec((blocks, 2 * chunk), lambda i: (0, i)),
            whole((2 * cell, 2 * cell)),
            whole((2 * cell, 2 * cell)),
            whole((2 * cell, 2 * cell)),
            whole((2 * cell, 2 * cell)),
            pl.BlockSpec((chunk, cell), lambda i: (i, 0)),
            pl.BlockSpec((chunk, cell), lambda i: (i, 0)),
        ],
        out_specs=whole((blocks, 2 * width)),
        scratch_shapes=[
            pltpu.VMEM((blocks, width), jnp.bfloat16),
            pltpu.VMEM((blocks, width), jnp.bfloat16),
            pltpu.VMEM((blocks, 2 * width), jnp.float32),
        ],
        cost_estimate=pl.CostEstimate(flops=flops, bytes_accessed=8 * 2**20, transcendentals=0),
        interpret=interpret,
    )(
        got, env, gain_row, fwd_hi, fwd_lo, back_hi, back_lo,
        inner_hi, inner_lo, outer_hi, outer_lo, jnp.cos(turn), jnp.sin(turn),
    )


def per_device(activation, filter_raw, decay_rate, skip_gain, grad_out, interpret=False):
    cell, model_width = activation.shape
    nx, nzh, ny, nzl, ncore = (lax.axis_size(n) for n in ("x", "zh", "y", "zl", "core"))
    flat = nx * ny * ncore
    deep = nzh * nzl
    blocks = flat * deep
    chan = model_width // blocks
    leaving = jnp.stack(
        [
            jnp.transpose(v).reshape(flat, deep, chan, cell)
            for v in (activation, filter_raw, grad_out)
        ],
        axis=2,
    )
    near = jnp.transpose(lax.all_to_all(leaving, plane, 0, 0), (1, 0, 2, 3, 4))
    got = lax.all_to_all(near, ring, 0, 0).reshape(blocks, 3 * chan * cell)
    row = jnp.arange(blocks, dtype=jnp.int32)
    core, row = row % ncore, row // ncore
    y, row = row % ny, row // ny
    x, row = row % nx, row // nx
    zl, zh = row % nzl, row // nzl
    places = (((zl * ncore + core) * nx + x) * nzh + zh) * ny + y
    first_chan = (lax.axis_index(plane) * deep + lax.axis_index(ring)) * chan
    rate = lax.dynamic_slice_in_dim(decay_rate, first_chan, chan)
    gain = lax.dynamic_slice_in_dim(skip_gain, first_chan, chan)
    done = local_part(got, rate, gain, places, chan, cell, blocks * cell, interpret)
    done = done.reshape(deep, flat, 2, chan, cell)
    far = jnp.transpose(lax.all_to_all(done, ring, 0, 0), (1, 0, 2, 3, 4))
    back = lax.all_to_all(far, plane, 0, 0).reshape(blocks, 2, chan, cell)
    return tuple(jnp.transpose(back[:, o].reshape(model_width, cell)) for o in range(2))


def solution(mesh, interpret=False):
    side = round(mesh.shape["seq"] ** (1 / 3))
    chips = mesh.devices.reshape(side, side, side, mesh.shape["sub"] // 2, 2)
    fine = jax.sharding.Mesh(chips, ("x", "zh", "y", "zl", "core"))
    split = P(tokens_over, None)
    return jax.shard_map(
        functools.partial(per_device, interpret=interpret),
        mesh=fine,
        in_specs=(split, split, P(), P(), split),
        out_specs=(split, split),
        check_vma=False,
    )
```

```python
import functools
import math

import jax
import jax.numpy as jnp
import numpy as np
from jax import lax
from jax.experimental import pallas as pl
from jax.experimental.pallas import tpu as pltpu
from jax.sharding import PartitionSpec as P

tokens_over = ("zl", "core", "x", "zh", "y")
plane = ("x", "y", "core")
ring = ("zh", "zl")


def table(values):
    high = values.astype(jnp.bfloat16)
    low = (values - high.astype(np.float64)).astype(jnp.bfloat16)
    return high, low


def halves(values):
    high = values.astype(jnp.bfloat16)
    return high, (values - high.astype(jnp.float32)).astype(jnp.bfloat16)


def mul(left, right):
    return jnp.dot(left, right, preferred_element_type=jnp.float32)


def mul_left(left, right):
    dims = (((0,), (0,)), ((), ()))
    return lax.dot_general(left, right, dims, preferred_element_type=jnp.float32)


def mul3(left, right):
    left_hi, left_lo = left
    right_hi, right_lo = right
    return mul(left_hi, right_hi) + (mul(left_hi, right_lo) + mul(left_lo, right_hi))


def correlate(
    chan, cell, chunk, scale,
    up_ref, raw_ref, act_ref, env_ref, gain_ref, fwd_hi_ref, fwd_lo_ref,
    inner_hi_ref, inner_lo_ref, outer_hi_ref, outer_lo_ref, cos_ref, sin_ref,
    through_ref, across_ref, taps_hi_ref, taps_lo_ref, total_ref,
):
    step = pl.program_id(0)
    width = chan * cell

    @pl.when(step == 0)
    def _():
        taps = raw_ref[...].astype(jnp.float32) * env_ref[...]
        high, low = halves(taps)
        taps_hi_ref[...] = high
        taps_lo_ref[...] = low
        total_ref[...] = jnp.zeros_like(total_ref)

    fwd_hi = fwd_hi_ref[...]
    fwd_lo = fwd_lo_ref[...]
    act = act_ref[...]
    up = up_ref[...]
    first = (
        mul(fwd_hi, act) + mul(fwd_lo, act),
        mul(fwd_hi, taps_hi_ref[...])
        + (mul(fwd_hi, taps_lo_ref[...]) + mul(fwd_lo, taps_hi_ref[...])),
        mul(fwd_hi, up) + mul(fwd_lo, up),
    )
    cosine = cos_ref[...]
    sine = sin_ref[...]
    inner = (inner_hi_ref[...], inner_lo_ref[...])
    outer = (outer_hi_ref[...], outer_lo_ref[...])
    spectra = []
    for values in first:
        rows = []
        for c in range(chan):
            re = values[:chunk, c * cell : (c + 1) * cell]
            im = values[chunk:, c * cell : (c + 1) * cell]
            rows.append(
                jnp.concatenate([re * cosine + im * sine, im * cosine - re * sine], axis=1)
            )
        spectra.append(mul3(halves(jnp.concatenate(rows, axis=0)), inner))
    up_re, up_im = spectra[2][:, :cell], spectra[2][:, cell:]
    parts_re, parts_im = [], []
    for other in (spectra[1], spectra[0]):
        re, im = other[:, :cell], other[:, cell:]
        mixed = jnp.concatenate([up_re * re + up_im * im, up_im * re - up_re * im], axis=1)
        back = mul3(halves(mixed), outer)
        for c in range(chan):
            zre = back[c * chunk : (c + 1) * chunk, :cell]
            zim = back[c * chunk : (c + 1) * chunk, cell:]
            parts_re.append(zre * cosine - zim * sine)
            parts_im.append(zim * cosine + zre * sine)
    spread = jnp.concatenate(
        [jnp.concatenate(parts_re, axis=1), jnp.concatenate(parts_im, axis=1)], axis=0
    )
    spread_hi, spread_lo = halves(spread)
    total_ref[...] += mul_left(fwd_hi, spread_hi) + (
        mul_left(fwd_hi, spread_lo) + mul_left(fwd_lo, spread_hi)
    )

    @pl.when(step == pl.num_programs(0) - 1)
    def _():
        through = total_ref[:, :width] * scale
        across = total_ref[:, width:] * scale
        up_float = up_ref[...].astype(jnp.float32)
        through_ref[...] = (through + gain_ref[...] * up_float).astype(jnp.bfloat16)
        across_ref[...] = (across * env_ref[...]).astype(jnp.bfloat16)


def local_part(up, raw, act, rate, gain, places, cell, total_tokens, interpret=False):
    blocks, width = up.shape
    chan = width // cell
    chunk = min(128, blocks)
    steps = blocks // chunk
    length = 2 * total_tokens
    odd = 2 * np.arange(blocks) + 1
    turns = 2.0 * math.pi * (odd[:, None] * places[None, :] % (4 * blocks)) / (4 * blocks)
    turns = turns.reshape(steps, 1, chunk, blocks)
    fwd = np.concatenate([np.cos(turns), -np.sin(turns)], 1).reshape(2 * blocks, blocks)
    fwd_hi, fwd_lo = table(fwd)
    cells = np.arange(cell)
    turns = 2.0 * math.pi * (cells[:, None] * cells[None, :] % cell) / cell
    inner = np.block([[np.cos(turns), -np.sin(turns)], [np.sin(turns), np.cos(turns)]])
    inner_hi, inner_lo = table(inner)
    outer_hi, outer_lo = table(inner.T)
    turns = 2.0 * math.pi * (odd[:, None] * cells[None, :]) / (2 * length)
    at = jnp.asarray(places[:, None] * cell + cells[None, :], jnp.float32)
    env = jnp.concatenate(
        [
            jnp.sqrt(2.0 * rate[c] / total_tokens) * jnp.exp(-(rate[c] * at) / total_tokens)
            for c in range(chan)
        ],
        1,
    )
    gain_row = jnp.repeat(gain, cell)[None, :]
    whole = lambda shape: pl.BlockSpec(shape, lambda i: (0, 0))
    flops = 2 * 3 * (5 * 2 * blocks * blocks * width + 5 * chan * blocks * 4 * cell * cell)
    return pl.pallas_call(
        functools.partial(correlate, chan, cell, chunk, 2.0 / length),
        grid=(steps,),
        out_shape=[jax.ShapeDtypeStruct((blocks, width), jnp.bfloat16)] * 2,
        in_specs=[whole((blocks, width))] * 4
        + [
            whole((1, width)),
            pl.BlockSpec((2 * chunk, blocks), lambda i: (i, 0)),
            pl.BlockSpec((2 * chunk, blocks), lambda i: (i, 0)),
        ]
        + [whole((2 * cell, 2 * cell))] * 4
        + [pl.BlockSpec((chunk, cell), lambda i: (i, 0))] * 2,
        out_specs=[whole((blocks, width))] * 2,
        scratch_shapes=[
            pltpu.VMEM((blocks, width), jnp.bfloat16),
            pltpu.VMEM((blocks, width), jnp.bfloat16),
            pltpu.VMEM((blocks, 2 * width), jnp.float32),
        ],
        cost_estimate=pl.CostEstimate(flops=flops, bytes_accessed=8 * 2**20, transcendentals=0),
        interpret=interpret,
    )(
        up, raw, act, env, gain_row, fwd_hi, fwd_lo, inner_hi, inner_lo, outer_hi, outer_lo,
        np.cos(turns).astype(np.float32), np.sin(turns).astype(np.float32),
    )


def place_of(names, sizes):
    at = 0
    for name in names:
        at = at * sizes[name] + lax.axis_index(name)
    return at


def device_at(names, sizes, at):
    where = {}
    for name in reversed(names):
        where[name] = lax.rem(at, sizes[name])
        at = lax.div(at, sizes[name])
    return where


def exchange_kernel(count, near, far, sizes, *refs):
    source, result, middle = refs[:count], refs[count : 2 * count], refs[2 * count : 3 * count]
    near_send, near_recv, far_send, far_recv, own = refs[3 * count :]
    near_count, far_count = source[0].shape[:2]
    near_at, far_at = place_of(near, sizes), place_of(far, sizes)
    barrier = pltpu.get_barrier_semaphore()

    def greet(names, at, total):
        def one(k, carry):
            peer = device_at(names, sizes, lax.rem(at + k, total))
            pl.semaphore_signal(
                barrier, inc=1, device_id=peer, device_id_type=pl.DeviceIdType.MESH
            )
            return carry

        lax.fori_loop(1, total, one, 0)

    greet(near, near_at, near_count)
    greet(far, far_at, far_count)
    pl.semaphore_wait(barrier, near_count + far_count - 2)

    def spread(names, at, total, piece, landing, send_sem, recv_sem):
        def one(k, carry):
            ahead = lax.div(k + 1, 2)
            to = lax.rem(at + jnp.where(lax.rem(k, 2) == 1, ahead, total - ahead), total)
            pltpu.make_async_remote_copy(
                src_ref=piece(to),
                dst_ref=landing,
                send_sem=send_sem,
                recv_sem=recv_sem,
                device_id=device_at(names, sizes, to),
                device_id_type=pl.DeviceIdType.MESH,
            ).start()
            return carry

        lax.fori_loop(1, total, one, 0)

    own_copies = []
    for i in range(count):
        spread(
            near, near_at, near_count, lambda to: source[i].at[to],
            middle[i].at[near_at], near_send.at[i], near_recv.at[i],
        )
        copy = pltpu.make_async_copy(source[i].at[near_at], middle[i].at[near_at], own.at[i])
        copy.start()
        own_copies.append(copy)
    for i in range(count):
        others = middle[i].at[pl.ds(0, near_count - 1)]
        pltpu.make_async_copy(others, others, near_recv.at[i]).wait()
        own_copies[i].wait()
        spread(
            far, far_at, far_count, lambda to: middle[i].at[:, to],
            result[i].at[far_at], far_send.at[i], far_recv.at[i],
        )
        copy = pltpu.make_async_copy(middle[i].at[:, far_at], result[i].at[far_at], own.at[i])
        copy.start()
        own_copies[i] = copy
    for i in range(count):
        own_copies[i].wait()
        others = source[i].at[pl.ds(0, near_count - 1)]
        pltpu.make_async_copy(others, others, near_send.at[i]).wait()
        others = result[i].at[pl.ds(0, far_count - 1)]
        pltpu.make_async_copy(others, others, far_send.at[i]).wait()
        pltpu.make_async_copy(others, others, far_recv.at[i]).wait()


def exchange(arrays, near, far, sizes, number, interpret):
    count = len(arrays)
    near_count, far_count, chan, cell = arrays[0].shape
    one = jax.ShapeDtypeStruct((far_count, near_count, chan, cell), arrays[0].dtype)
    return pl.pallas_call(
        functools.partial(exchange_kernel, count, near, far, sizes),
        out_shape=[one] * count,
        in_specs=[pl.BlockSpec(memory_space=pltpu.VMEM)] * count,
        out_specs=[pl.BlockSpec(memory_space=pltpu.VMEM)] * count,
        scratch_shapes=[pltpu.VMEM(arrays[0].shape, arrays[0].dtype)] * count
        + [pltpu.SemaphoreType.DMA((count,))] * 5,
        compiler_params=pltpu.CompilerParams(collective_id=number, has_side_effects=True),
        interpret=interpret,
    )(*arrays)


def per_device(sizes, activation, filter_raw, decay_rate, skip_gain, grad_out, interpret=False):
    cell, model_width = activation.shape
    flat = math.prod(sizes[n] for n in plane)
    deep = math.prod(sizes[n] for n in ring)
    blocks = flat * deep
    chan = model_width // blocks
    leaving = [
        jnp.transpose(v).reshape(flat, deep, chan, cell)
        for v in (grad_out, filter_raw, activation)
    ]
    got = exchange(leaving, plane, ring, sizes, 0, interpret and pltpu.InterpretParams())
    row = np.arange(blocks)
    at = {}
    for name in reversed(ring + plane):
        at[name] = row % sizes[name]
        row = row // sizes[name]
    places = 0
    for name in tokens_over:
        places = places * sizes[name] + at[name]
    first_chan = (lax.axis_index(plane) * deep + lax.axis_index(ring)) * chan
    rate = lax.dynamic_slice_in_dim(decay_rate, first_chan, chan)
    gain = lax.dynamic_slice_in_dim(skip_gain, first_chan, chan)
    up, raw, act = (v.reshape(blocks, chan * cell) for v in got)
    done = local_part(up, raw, act, rate, gain, places, cell, blocks * cell, bool(interpret))
    done = [v.reshape(deep, flat, chan, cell) for v in done]
    back = exchange(done, ring, plane, sizes, 1, interpret and pltpu.InterpretParams())
    return tuple(jnp.transpose(v.reshape(model_width, cell)) for v in back)


def solution(mesh, interpret=False):
    side = round(mesh.shape["seq"] ** (1 / 3))
    chips = mesh.devices.reshape(side, side, side, mesh.shape["sub"] // 2, 2)
    fine = jax.sharding.Mesh(chips, ("x", "zh", "y", "zl", "core"))
    split = P(tokens_over, None)
    return jax.shard_map(
        functools.partial(per_device, dict(fine.shape), interpret=interpret),
        mesh=fine,
        in_specs=(split, split, P(), P(), split),
        out_specs=(split, split),
        check_vma=False,
    )
```

```python
import functools
import math

import jax
import jax.numpy as jnp
import numpy as np
from jax import lax
from jax.experimental import pallas as pl
from jax.experimental.pallas import tpu as pltpu
from jax.sharding import PartitionSpec as P

tokens_over = ("zl", "core", "x", "zh", "y")
plane = ("x", "y", "core")
ring = ("zh", "zl")


def table(values):
    high = values.astype(jnp.bfloat16)
    low = (values - high.astype(np.float64)).astype(jnp.bfloat16)
    return high, low


def halves(values):
    high = values.astype(jnp.bfloat16)
    return high, (values - high.astype(jnp.float32)).astype(jnp.bfloat16)


def mul(left, right):
    return jnp.dot(left, right, preferred_element_type=jnp.float32)


def mul_left(left, right):
    dims = (((0,), (0,)), ((), ()))
    return lax.dot_general(left, right, dims, preferred_element_type=jnp.float32)


def mul3(left, right):
    left_hi, left_lo = left
    right_hi, right_lo = right
    return mul(left_hi, right_hi) + (mul(left_hi, right_lo) + mul(left_lo, right_hi))


def place_of(names, sizes):
    at = 0
    for name in names:
        at = at * sizes[name] + lax.axis_index(name)
    return at


def device_at(names, sizes, at):
    where = {}
    for name in reversed(names):
        where[name] = lax.rem(at, sizes[name])
        at = lax.div(at, sizes[name])
    return where


def fused_kernel(
    sizes, chunk,
    up_ref, raw_ref, act_ref, rate_ref, gain_ref, at_ref, fwd_hi_ref, fwd_lo_ref,
    inner_hi_ref, inner_lo_ref, outer_hi_ref, outer_lo_ref, cos_ref, sin_ref,
    through_ref, across_ref,
    mid_up, mid_raw, mid_act, got_up, got_raw, got_act, done_through, done_across,
    mid_through, mid_across, spec_ref, total_ref, env_ref, taps_hi_ref, taps_lo_ref,
    flat_send, flat_recv, deep_send, deep_recv, flat_own, deep_own,
):
    flat, deep, chan, cell = up_ref.shape
    blocks, width = flat * deep, chan * cell
    steps = blocks // chunk
    tokens = blocks * cell
    flat_at, deep_at = place_of(plane, sizes), place_of(ring, sizes)
    barrier = pltpu.get_barrier_semaphore()
    mesh_id = pl.DeviceIdType.MESH

    def greet(names, at, count):
        def one(k, carry):
            peer = device_at(names, sizes, lax.rem(at + k, count))
            pl.semaphore_signal(barrier, inc=1, device_id=peer, device_id_type=mesh_id)
            return carry

        lax.fori_loop(1, count, one, 0)

    greet(plane, flat_at, flat)
    greet(ring, deep_at, deep)
    pl.semaphore_wait(barrier, flat + deep - 2)

    def spread(names, at, count, piece, landing, send_sem, recv_sem, own_sem):
        def one(k, carry):
            ahead = lax.div(k + 1, 2)
            to = lax.rem(at + jnp.where(lax.rem(k, 2) == 1, ahead, count - ahead), count)
            pltpu.make_async_remote_copy(
                src_ref=piece(to),
                dst_ref=landing,
                send_sem=send_sem,
                recv_sem=recv_sem,
                device_id=device_at(names, sizes, to),
                device_id_type=mesh_id,
            ).start()
            return carry

        lax.fori_loop(1, count, one, 0)
        own = pltpu.make_async_copy(piece(at), landing, own_sem)
        own.start()
        return own

    def settle(ref, count, sem):
        others = ref.at[pl.ds(0, count - 1)]
        pltpu.make_async_copy(others, others, sem).wait()

    def over_plane(i, piece, landing):
        return spread(
            plane, flat_at, flat, piece, landing, flat_send.at[i], flat_recv.at[i], flat_own.at[i]
        )

    def over_ring(i, piece, landing):
        return spread(
            ring, deep_at, deep, piece, landing, deep_send.at[i], deep_recv.at[i], deep_own.at[i]
        )

    leaving = (up_ref, raw_ref, act_ref)
    middle = (mid_up, mid_raw, mid_act)
    got = (got_up, got_raw, got_act)
    own_flat = [
        over_plane(i, lambda to: leaving[i].at[to], middle[i].at[flat_at]) for i in range(3)
    ]
    first_chan = (flat_at * deep + deep_at) * chan
    at = at_ref[...]
    for c in range(chan):
        rate = jnp.full((1, cell), rate_ref[first_chan + c], jnp.float32)
        env_ref[:, c * cell : (c + 1) * cell] = jnp.sqrt(2.0 * rate / tokens) * jnp.exp(
            -(rate * at) / tokens
        )
    own_deep = []
    for i in range(3):
        settle(middle[i], flat, flat_recv.at[i])
        own_flat[i].wait()
        own_deep.append(
            over_ring(i, lambda to: middle[i].at[:, to], got[i].at[deep_at])
        )

    inner = (inner_hi_ref[...], inner_lo_ref[...])
    outer = (outer_hi_ref[...], outer_lo_ref[...])

    def arrived(i):
        settle(got[i], deep, deep_recv.at[i])
        own_deep[i].wait()
        return got[i][...].reshape(blocks, width)

    def tables(s):
        rows = pl.ds(pl.multiple_of(s * 2 * chunk, 2 * chunk), 2 * chunk)
        few = pl.ds(pl.multiple_of(s * chunk, chunk), chunk)
        return fwd_hi_ref[rows, :], fwd_lo_ref[rows, :], cos_ref[few, :], sin_ref[few, :]

    def forward(values, cosine, sine):
        rows = []
        for c in range(chan):
            re = values[:chunk, c * cell : (c + 1) * cell]
            im = values[chunk:, c * cell : (c + 1) * cell]
            rows.append(
                jnp.concatenate([re * cosine + im * sine, im * cosine - re * sine], axis=1)
            )
        return mul3(halves(jnp.concatenate(rows, axis=0)), inner)

    def inverse(s, other, fwd_hi, fwd_lo, cosine, sine):
        ahead = spec_ref[s]
        up_re, up_im = ahead[:, :cell], ahead[:, cell:]
        re, im = other[:, :cell], other[:, cell:]
        mixed = jnp.concatenate([up_re * re + up_im * im, up_im * re - up_re * im], axis=1)
        back = mul3(halves(mixed), outer)
        parts_re, parts_im = [], []
        for c in range(chan):
            zre = back[c * chunk : (c + 1) * chunk, :cell]
            zim = back[c * chunk : (c + 1) * chunk, cell:]
            parts_re.append(zre * cosine - zim * sine)
            parts_im.append(zim * cosine + zre * sine)
        spread_hi, spread_lo = halves(
            jnp.concatenate(
                [jnp.concatenate(parts_re, axis=1), jnp.concatenate(parts_im, axis=1)], axis=0
            )
        )
        total_ref[...] += mul_left(fwd_hi, spread_hi) + (
            mul_left(fwd_hi, spread_lo) + mul_left(fwd_lo, spread_hi)
        )

    taps_hi_ref[...] = arrived(0)

    def up_step(s, carry):
        fwd_hi, fwd_lo, cosine, sine = tables(s)
        up = taps_hi_ref[...]
        spec_ref[s] = forward(mul(fwd_hi, up) + mul(fwd_lo, up), cosine, sine)
        return carry

    lax.fori_loop(0, steps, up_step, 0)

    taps_hi, taps_lo = halves(arrived(1).astype(jnp.float32) * env_ref[...])
    taps_hi_ref[...] = taps_hi
    taps_lo_ref[...] = taps_lo
    total_ref[...] = jnp.zeros_like(total_ref)

    def taps_step(s, carry):
        fwd_hi, fwd_lo, cosine, sine = tables(s)
        high = taps_hi_ref[...]
        first = mul(fwd_hi, high) + (mul(fwd_hi, taps_lo_ref[...]) + mul(fwd_lo, high))
        inverse(s, forward(first, cosine, sine), fwd_hi, fwd_lo, cosine, sine)
        return carry

    lax.fori_loop(0, steps, taps_step, 0)
    scale = 1.0 / tokens
    up_float = got_up[...].reshape(blocks, width).astype(jnp.float32)
    gain = jnp.concatenate(
        [jnp.full((1, cell), gain_ref[first_chan + c], jnp.float32) for c in range(chan)], axis=1
    )
    through = (total_ref[...] * scale + gain * up_float).astype(jnp.bfloat16)
    done_through[...] = through.reshape(done_through.shape)
    own_deep.append(
        over_ring(3, lambda to: done_through.at[to], mid_through.at[deep_at])
    )

    taps_hi_ref[...] = arrived(2)
    total_ref[...] = jnp.zeros_like(total_ref)

    def act_step(s, carry):
        fwd_hi, fwd_lo, cosine, sine = tables(s)
        act = taps_hi_ref[...]
        first = mul(fwd_hi, act) + mul(fwd_lo, act)
        inverse(s, forward(first, cosine, sine), fwd_hi, fwd_lo, cosine, sine)
        return carry

    lax.fori_loop(0, steps, act_step, 0)
    across = (total_ref[...] * scale * env_ref[...]).astype(jnp.bfloat16)
    done_across[...] = across.reshape(done_across.shape)
    own_deep.append(
        over_ring(4, lambda to: done_across.at[to], mid_across.at[deep_at])
    )
    leaving = leaving + (done_through, done_across)
    middle = middle + (mid_through, mid_across)
    final = (through_ref, across_ref)
    for i in range(2):
        settle(middle[3 + i], deep, deep_recv.at[3 + i])
        own_deep[3 + i].wait()
        own_flat.append(
            over_plane(3 + i, lambda to: middle[3 + i].at[:, to], final[i].at[flat_at])
        )
    for i in range(3):
        settle(leaving[i], flat, flat_send.at[i])
        settle(got[i], deep, deep_send.at[i])
    for i in range(2):
        settle(done_through, deep, deep_send.at[3 + i])
        settle(final[i], flat, flat_send.at[3 + i])
        settle(final[i], flat, flat_recv.at[3 + i])
        own_flat[3 + i].wait()


def fused(leaving, decay_rate, skip_gain, places, sizes, interpret):
    flat, deep, chan, cell = leaving[0].shape
    blocks, width = flat * deep, chan * cell
    chunk = min(128, blocks)
    steps = blocks // chunk
    length = 2 * blocks * cell
    odd = 2 * np.arange(blocks) + 1
    turns = 2.0 * math.pi * (odd[:, None] * places[None, :] % (4 * blocks)) / (4 * blocks)
    turns = turns.reshape(steps, 1, chunk, blocks)
    fwd = np.concatenate([np.cos(turns), -np.sin(turns)], 1).reshape(2 * blocks, blocks)
    fwd_hi, fwd_lo = table(fwd)
    cells = np.arange(cell)
    turns = 2.0 * math.pi * (cells[:, None] * cells[None, :] % cell) / cell
    inner = np.block([[np.cos(turns), -np.sin(turns)], [np.sin(turns), np.cos(turns)]])
    inner_hi, inner_lo = table(inner)
    outer_hi, outer_lo = table(inner.T)
    turns = 2.0 * math.pi * (odd[:, None] * cells[None, :]) / (2 * length)
    at = (places[:, None] * cell + cells[None, :]).astype(np.float32)
    near = pltpu.VMEM((flat, deep, chan, cell), jnp.bfloat16)
    far = pltpu.VMEM((deep, flat, chan, cell), jnp.bfloat16)
    vmem = pl.BlockSpec(memory_space=pltpu.VMEM)
    smem = pl.BlockSpec(memory_space=pltpu.SMEM)
    return pl.pallas_call(
        functools.partial(fused_kernel, sizes, chunk),
        out_shape=[jax.ShapeDtypeStruct(leaving[0].shape, jnp.bfloat16)] * 2,
        in_specs=[vmem] * 3 + [smem] * 2 + [vmem] * 9,
        out_specs=[vmem] * 2,
        scratch_shapes=[near] * 3
        + [far] * 7
        + [
            pltpu.VMEM((steps, chan * chunk, 2 * cell), jnp.float32),
            pltpu.VMEM((blocks, width), jnp.float32),
            pltpu.VMEM((blocks, width), jnp.float32),
            pltpu.VMEM((blocks, width), jnp.bfloat16),
            pltpu.VMEM((blocks, width), jnp.bfloat16),
        ]
        + [pltpu.SemaphoreType.DMA((5,))] * 6,
        compiler_params=pltpu.CompilerParams(collective_id=0, has_side_effects=True),
        interpret=interpret,
    )(
        *leaving, decay_rate, skip_gain, at, fwd_hi, fwd_lo, inner_hi, inner_lo, outer_hi,
        outer_lo, np.cos(turns).astype(np.float32), np.sin(turns).astype(np.float32),
    )


def per_device(sizes, activation, filter_raw, decay_rate, skip_gain, grad_out, interpret=False):
    cell, model_width = activation.shape
    flat = math.prod(sizes[n] for n in plane)
    deep = math.prod(sizes[n] for n in ring)
    blocks = flat * deep
    chan = model_width // blocks
    leaving = [
        jnp.transpose(v).reshape(flat, deep, chan, cell)
        for v in (grad_out, filter_raw, activation)
    ]
    row = np.arange(blocks)
    at = {}
    for name in reversed(ring + plane):
        at[name] = row % sizes[name]
        row = row // sizes[name]
    places = 0
    for name in tokens_over:
        places = places * sizes[name] + at[name]
    back = fused(
        leaving, decay_rate, skip_gain, places, sizes, interpret and pltpu.InterpretParams()
    )
    return tuple(jnp.transpose(v.reshape(model_width, cell)) for v in back)


def solution(mesh, interpret=False):
    side = round(mesh.shape["seq"] ** (1 / 3))
    chips = mesh.devices.reshape(side, side, side, mesh.shape["sub"] // 2, 2)
    fine = jax.sharding.Mesh(chips, ("x", "zh", "y", "zl", "core"))
    split = P(tokens_over, None)
    return jax.shard_map(
        functools.partial(per_device, dict(fine.shape), interpret=interpret),
        mesh=fine,
        in_specs=(split, split, P(), P(), split),
        out_specs=(split, split),
        check_vma=False,
    )
```

```python
import functools
import math

import jax
import jax.numpy as jnp
import numpy as np
from jax import lax
from jax.experimental import pallas as pl
from jax.experimental.pallas import tpu as pltpu
from jax.sharding import PartitionSpec as P

tokens_over = ("zl", "core", "x", "zh", "y")
plane = ("core", "x", "y")
ring = ("zl", "zh")


def table(values):
    high = values.astype(jnp.bfloat16)
    low = (values - high.astype(np.float64)).astype(jnp.bfloat16)
    return high, low


def halves(values):
    high = values.astype(jnp.bfloat16)
    return high, (values - high.astype(jnp.float32)).astype(jnp.bfloat16)


def mul(left, right):
    return jnp.dot(left, right, preferred_element_type=jnp.float32)


def mul_left(left, right):
    dims = (((0,), (0,)), ((), ()))
    return lax.dot_general(left, right, dims, preferred_element_type=jnp.float32)


def mul3(left, right):
    left_hi, left_lo = left
    right_hi, right_lo = right
    return mul(left_hi, right_hi) + (mul(left_hi, right_lo) + mul(left_lo, right_hi))


def place_of(names, sizes):
    at = 0
    for name in names:
        at = at * sizes[name] + lax.axis_index(name)
    return at


def device_at(names, sizes, at):
    where = {}
    for name in reversed(names):
        where[name] = lax.rem(at, sizes[name])
        at = lax.div(at, sizes[name])
    return where


def fused_kernel(
    sizes, chunk,
    up_ref, raw_ref, act_ref, rate_ref, gain_ref, at_ref, fwd_hi_far, fwd_lo_far,
    inner_hi_ref, inner_lo_ref, outer_hi_ref, outer_lo_ref, cos_ref, sin_ref,
    through_ref, across_ref,
    out_up, out_raw, out_act, mid_up, mid_raw, mid_act, got_up, got_raw, got_act, done_through, done_across,
    mid_through, mid_across, spec_ref, total_ref, env_ref, taps_hi_ref, taps_lo_ref,
    fwd_hi_ref, fwd_lo_ref, flat_send, flat_recv, deep_send, deep_recv, held_sem,
):
    flat, deep, chan, cell = out_up.shape
    blocks, width = flat * deep, chan * cell
    steps = blocks // chunk
    tokens = blocks * cell
    flat_at, deep_at = place_of(plane, sizes), place_of(ring, sizes)
    barrier = pltpu.get_barrier_semaphore()
    mesh_id = pl.DeviceIdType.MESH

    def greet(names, at, count):
        def one(k, carry):
            peer = device_at(names, sizes, lax.rem(at + k, count))
            pl.semaphore_signal(barrier, inc=1, device_id=peer, device_id_type=mesh_id)
            return carry

        lax.fori_loop(1, count, one, 0)

    greet(plane, flat_at, flat)
    greet(ring, deep_at, deep)
    held = [
        pltpu.make_async_copy(fwd_hi_far, fwd_hi_ref, held_sem.at[0]),
        pltpu.make_async_copy(fwd_lo_far, fwd_lo_ref, held_sem.at[1]),
    ]
    for copy in held:
        copy.start()
    for given, turned in ((up_ref, out_up), (raw_ref, out_raw), (act_ref, out_act)):
        turned[...] = jnp.transpose(given[...]).reshape(turned.shape)
    pl.semaphore_wait(barrier, flat + deep - 2)

    parts = (2, 1, 1, 1, 2)

    def spread(names, at, low, count, piece, landing, send_sem, recv_sem):
        def one(k, carry):
            to = low + lax.rem(at + k, count)

            @pl.when(to != at)
            def _():
                pltpu.make_async_remote_copy(
                    src_ref=piece(to),
                    dst_ref=landing,
                    send_sem=send_sem,
                    recv_sem=recv_sem,
                    device_id=device_at(names, sizes, to),
                    device_id_type=mesh_id,
                ).start()

            @pl.when(to == at)
            def _():
                pltpu.make_async_copy(piece(at), landing, recv_sem).start()

            return carry

        lax.fori_loop(1, count + 1, one, 0)

    def settle(ref, sem):
        pltpu.make_async_copy(ref, ref, sem).wait()

    def cut(i, h, count):
        return pl.ds(h * (count // parts[i]), count // parts[i])

    def first_stage(i, names, at, count, other, send_sem, recv_sem):
        for h in range(parts[i]):
            rows = cut(i, h, other)
            spread(
                names, at, 0, count, lambda to: leaving[i].at[to, rows],
                middle[i].at[at, rows], send_sem.at[i], recv_sem.at[i, h],
            )

    def second_stage(i, names, at, count, waited, send_sem, recv_sem):
        for h in range(parts[i]):
            settle(middle[i].at[:, cut(i, h, count)], waited.at[i, h])
            size = count // parts[i]
            spread(
                names, at, h * size, size, lambda to: middle[i].at[:, to],
                landed[i].at[at], send_sem.at[i], recv_sem.at[i, 0],
            )

    leaving = (out_up, out_raw, out_act, done_through, done_across)
    middle = (mid_up, mid_raw, mid_act, mid_through, mid_across)
    landed = (got_up, got_raw, got_act, through_ref, across_ref)
    for i in range(3):
        first_stage(i, plane, flat_at, flat, deep, flat_send, flat_recv)
    first_chan = (flat_at * deep + deep_at) * chan
    at = at_ref[...]
    for c in range(chan):
        rate = jnp.full((1, cell), rate_ref[first_chan + c], jnp.float32)
        env_ref[:, c * cell : (c + 1) * cell] = jnp.sqrt(2.0 * rate / tokens) * jnp.exp(
            -(rate * at) / tokens
        )
    for i in range(3):
        second_stage(i, ring, deep_at, deep, flat_recv, deep_send, deep_recv)
    for copy in held:
        copy.wait()

    inner = (inner_hi_ref[...], inner_lo_ref[...])
    outer = (outer_hi_ref[...], outer_lo_ref[...])

    def arrived(i):
        settle(landed[i], deep_recv.at[i, 0])
        return landed[i][...].reshape(blocks, width)

    def tables(s):
        rows = pl.ds(pl.multiple_of(s * 2 * chunk, 2 * chunk), 2 * chunk)
        few = pl.ds(pl.multiple_of(s * chunk, chunk), chunk)
        return fwd_hi_ref[rows, :], fwd_lo_ref[rows, :], cos_ref[few, :], sin_ref[few, :]

    def forward(values, cosine, sine):
        rows = []
        for c in range(chan):
            re = values[:chunk, c * cell : (c + 1) * cell]
            im = values[chunk:, c * cell : (c + 1) * cell]
            rows.append(
                jnp.concatenate([re * cosine + im * sine, im * cosine - re * sine], axis=1)
            )
        return mul3(halves(jnp.concatenate(rows, axis=0)), inner)

    def inverse(s, other, fwd_hi, fwd_lo, cosine, sine):
        ahead = spec_ref[s]
        up_re, up_im = ahead[:, :cell], ahead[:, cell:]
        re, im = other[:, :cell], other[:, cell:]
        mixed = jnp.concatenate([up_re * re + up_im * im, up_im * re - up_re * im], axis=1)
        back = mul3(halves(mixed), outer)
        parts_re, parts_im = [], []
        for c in range(chan):
            zre = back[c * chunk : (c + 1) * chunk, :cell]
            zim = back[c * chunk : (c + 1) * chunk, cell:]
            parts_re.append(zre * cosine - zim * sine)
            parts_im.append(zim * cosine + zre * sine)
        spread_hi, spread_lo = halves(
            jnp.concatenate(
                [jnp.concatenate(parts_re, axis=1), jnp.concatenate(parts_im, axis=1)], axis=0
            )
        )
        total_ref[...] += mul_left(fwd_hi, spread_hi) + (
            mul_left(fwd_hi, spread_lo) + mul_left(fwd_lo, spread_hi)
        )

    taps_hi_ref[...] = arrived(0)

    def up_step(s, carry):
        fwd_hi, fwd_lo, cosine, sine = tables(s)
        up = taps_hi_ref[...]
        spec_ref[s] = forward(mul(fwd_hi, up) + mul(fwd_lo, up), cosine, sine)
        return carry

    lax.fori_loop(0, steps, up_step, 0)

    taps_hi, taps_lo = halves(arrived(1).astype(jnp.float32) * env_ref[...])
    taps_hi_ref[...] = taps_hi
    taps_lo_ref[...] = taps_lo
    total_ref[...] = jnp.zeros_like(total_ref)

    def taps_step(s, carry):
        fwd_hi, fwd_lo, cosine, sine = tables(s)
        high = taps_hi_ref[...]
        first = mul(fwd_hi, high) + (mul(fwd_hi, taps_lo_ref[...]) + mul(fwd_lo, high))
        inverse(s, forward(first, cosine, sine), fwd_hi, fwd_lo, cosine, sine)
        return carry

    lax.fori_loop(0, steps, taps_step, 0)
    scale = 1.0 / tokens
    up_float = got_up[...].reshape(blocks, width).astype(jnp.float32)
    gain = jnp.concatenate(
        [jnp.full((1, cell), gain_ref[first_chan + c], jnp.float32) for c in range(chan)], axis=1
    )
    through = (total_ref[...] * scale + gain * up_float).astype(jnp.bfloat16)
    done_through[...] = through.reshape(done_through.shape)
    first_stage(3, ring, deep_at, deep, flat, deep_send, deep_recv)

    taps_hi_ref[...] = arrived(2)
    total_ref[...] = jnp.zeros_like(total_ref)

    def act_step(s, carry):
        fwd_hi, fwd_lo, cosine, sine = tables(s)
        act = taps_hi_ref[...]
        first = mul(fwd_hi, act) + mul(fwd_lo, act)
        inverse(s, forward(first, cosine, sine), fwd_hi, fwd_lo, cosine, sine)
        return carry

    lax.fori_loop(0, steps, act_step, 0)
    across = (total_ref[...] * scale * env_ref[...]).astype(jnp.bfloat16)
    done_across[...] = across.reshape(done_across.shape)
    first_stage(4, ring, deep_at, deep, flat, deep_send, deep_recv)
    for i in (3, 4):
        second_stage(i, plane, flat_at, flat, deep_recv, flat_send, flat_recv)
    for i in range(5):
        first_send, last_send = (flat_send, deep_send) if i < 3 else (deep_send, flat_send)
        settle(leaving[i].at[pl.ds(0, leaving[i].shape[0] - 1)], first_send.at[i])
        settle(landed[i].at[pl.ds(0, landed[i].shape[0] - 1)], last_send.at[i])
    for i in (3, 4):
        settle(landed[i], flat_recv.at[i, 0])


def fused(given, decay_rate, skip_gain, places, flat, deep, sizes, interpret):
    cell = given[0].shape[0]
    chan = given[0].shape[1] // (flat * deep)
    blocks, width = flat * deep, chan * cell
    chunk = min(128, blocks)
    steps = blocks // chunk
    length = 2 * blocks * cell
    odd = 2 * np.arange(blocks) + 1
    turns = 2.0 * math.pi * (odd[:, None] * places[None, :] % (4 * blocks)) / (4 * blocks)
    turns = turns.reshape(steps, 1, chunk, blocks)
    fwd = np.concatenate([np.cos(turns), -np.sin(turns)], 1).reshape(2 * blocks, blocks)
    fwd_hi, fwd_lo = table(fwd)
    cells = np.arange(cell)
    turns = 2.0 * math.pi * (cells[:, None] * cells[None, :] % cell) / cell
    inner = np.block([[np.cos(turns), -np.sin(turns)], [np.sin(turns), np.cos(turns)]])
    inner_hi, inner_lo = table(inner)
    outer_hi, outer_lo = table(inner.T)
    turns = 2.0 * math.pi * (odd[:, None] * cells[None, :]) / (2 * length)
    at = (places[:, None] * cell + cells[None, :]).astype(np.float32)
    near = pltpu.VMEM((flat, deep, chan, cell), jnp.bfloat16)
    far = pltpu.VMEM((deep, flat, chan, cell), jnp.bfloat16)
    vmem = pl.BlockSpec(memory_space=pltpu.VMEM)
    smem = pl.BlockSpec(memory_space=pltpu.SMEM)
    return pl.pallas_call(
        functools.partial(fused_kernel, sizes, chunk),
        out_shape=[jax.ShapeDtypeStruct((flat, deep, chan, cell), jnp.bfloat16)] * 2,
        in_specs=[vmem] * 3 + [smem] * 2 + [vmem] + [pl.BlockSpec(memory_space=pl.ANY)] * 2 + [vmem] * 6,
        out_specs=[vmem] * 2,
        scratch_shapes=[near] * 6
        + [far] * 7
        + [
            pltpu.VMEM((steps, chan * chunk, 2 * cell), jnp.float32),
            pltpu.VMEM((blocks, width), jnp.float32),
            pltpu.VMEM((blocks, width), jnp.float32),
            pltpu.VMEM((blocks, width), jnp.bfloat16),
            pltpu.VMEM((blocks, width), jnp.bfloat16),
            pltpu.VMEM((2 * blocks, blocks), jnp.bfloat16),
            pltpu.VMEM((2 * blocks, blocks), jnp.bfloat16),
        ]
        + [pltpu.SemaphoreType.DMA((5,)), pltpu.SemaphoreType.DMA((5, 2))] * 2
        + [pltpu.SemaphoreType.DMA((2,))],
        compiler_params=pltpu.CompilerParams(collective_id=0, has_side_effects=True),
        interpret=interpret,
    )(
        *given, decay_rate, skip_gain, at, fwd_hi, fwd_lo, inner_hi, inner_lo, outer_hi,
        outer_lo, np.cos(turns).astype(np.float32), np.sin(turns).astype(np.float32),
    )


def per_device(sizes, activation, filter_raw, decay_rate, skip_gain, grad_out, interpret=False):
    cell, model_width = activation.shape
    flat = math.prod(sizes[n] for n in plane)
    deep = math.prod(sizes[n] for n in ring)
    blocks = flat * deep
    row = np.arange(blocks)
    at = {}
    for name in reversed(ring + plane):
        at[name] = row % sizes[name]
        row = row // sizes[name]
    places = 0
    for name in tokens_over:
        places = places * sizes[name] + at[name]
    back = fused(
        (grad_out, filter_raw, activation), decay_rate, skip_gain, places, flat, deep, sizes,
        interpret and pltpu.InterpretParams(),
    )
    return tuple(jnp.transpose(v.reshape(model_width, cell)) for v in back)


def solution(mesh, interpret=False):
    side = round(mesh.shape["seq"] ** (1 / 3))
    chips = mesh.devices.reshape(side, side, side, mesh.shape["sub"] // 2, 2)
    fine = jax.sharding.Mesh(chips, ("x", "zh", "y", "zl", "core"))
    split = P(tokens_over, None)
    return jax.shard_map(
        functools.partial(per_device, dict(fine.shape), interpret=interpret),
        mesh=fine,
        in_specs=(split, split, P(), P(), split),
        out_specs=(split, split),
        check_vma=False,
    )
```

```python
import functools
import math

import jax
import jax.numpy as jnp
import numpy as np
from jax import lax
from jax.experimental import pallas as pl
from jax.experimental.pallas import tpu as pltpu
from jax.sharding import PartitionSpec as P

tokens_over = ("zl", "core", "x", "zh", "y")
plane = ("core", "x", "y")
ring = ("zl", "zh")


def table(values):
    high = values.astype(jnp.bfloat16)
    low = (values - high.astype(np.float64)).astype(jnp.bfloat16)
    return high, low


def halves(values):
    high = values.astype(jnp.bfloat16)
    return high, (values - high.astype(jnp.float32)).astype(jnp.bfloat16)


def mul(left, right):
    return jnp.dot(left, right, preferred_element_type=jnp.float32)


def mul_left(left, right):
    dims = (((0,), (0,)), ((), ()))
    return lax.dot_general(left, right, dims, preferred_element_type=jnp.float32)


def mul3(left, right):
    left_hi, left_lo = left
    right_hi, right_lo = right
    return mul(left_hi, right_hi) + (mul(left_hi, right_lo) + mul(left_lo, right_hi))


def place_of(names, sizes):
    at = 0
    for name in names:
        at = at * sizes[name] + lax.axis_index(name)
    return at


def device_at(names, sizes, at):
    where = {}
    for name in reversed(names):
        where[name] = lax.rem(at, sizes[name])
        at = lax.div(at, sizes[name])
    return where


def fused_kernel(
    sizes, chunk,
    up_ref, raw_ref, act_ref, rate_ref, gain_ref, at_ref, fwd_hi_far, fwd_lo_far,
    inner_hi_ref, inner_lo_ref, outer_hi_ref, outer_lo_ref, cos_ref, sin_ref,
    through_ref, across_ref,
    out_up, out_raw, out_act, mid_up, mid_raw, mid_act, got_up, got_raw, got_act, done_through, done_across,
    mid_through, mid_across, spec_ref, total_ref, env_ref, taps_hi_ref, taps_lo_ref,
    fwd_hi_ref, fwd_lo_ref, flat_send, flat_recv, deep_send, deep_recv, held_sem,
):
    flat, deep, chan, cell = out_up.shape
    blocks, width = flat * deep, chan * cell
    steps = blocks // chunk
    tokens = blocks * cell
    flat_at, deep_at = place_of(plane, sizes), place_of(ring, sizes)
    barrier = pltpu.get_barrier_semaphore()
    mesh_id = pl.DeviceIdType.MESH

    def greet(names, at, count):
        def one(k, carry):
            peer = device_at(names, sizes, lax.rem(at + k, count))
            pl.semaphore_signal(barrier, inc=1, device_id=peer, device_id_type=mesh_id)
            return carry

        lax.fori_loop(1, count, one, 0)

    greet(plane, flat_at, flat)
    greet(ring, deep_at, deep)
    held = [
        pltpu.make_async_copy(fwd_hi_far, fwd_hi_ref, held_sem.at[0]),
        pltpu.make_async_copy(fwd_lo_far, fwd_lo_ref, held_sem.at[1]),
    ]
    for copy in held:
        copy.start()
    for given, turned in ((up_ref, out_up), (raw_ref, out_raw), (act_ref, out_act)):
        turned[...] = jnp.transpose(given[...]).reshape(turned.shape)
    pl.semaphore_wait(barrier, flat + deep - 2)

    halves_x = 2 - sizes["x"] % 2
    parts = (sizes["zl"], 1, 1, 1, 2 * halves_x)
    half_at = lax.div(lax.axis_index("x"), sizes["x"] // halves_x)

    def spread(names, at, low, count, piece, landing, send_sem, recv_sem):
        def one(k, carry):
            to = low + lax.rem(at + k, count)

            @pl.when(to != at)
            def _():
                pltpu.make_async_remote_copy(
                    src_ref=piece(to),
                    dst_ref=landing,
                    send_sem=send_sem,
                    recv_sem=recv_sem,
                    device_id=device_at(names, sizes, to),
                    device_id_type=mesh_id,
                ).start()

            @pl.when(to == at)
            def _():
                pltpu.make_async_copy(piece(at), landing, recv_sem).start()

            return carry

        lax.fori_loop(1, count + 1, one, 0)

    def settle(ref, sem):
        pltpu.make_async_copy(ref, ref, sem).wait()

    def cut(i, h, count):
        size = count // parts[i]
        slot = 0
        if i == 0:
            slot = lax.rem(lax.axis_index("zl") + h, sizes["zl"])
        if i == 4:
            core = lax.rem(lax.axis_index("core") + 1 - h // halves_x, 2)
            half = lax.rem(half_at + halves_x - 1 - h % halves_x, halves_x)
            slot = core * halves_x + half
        return slot * size, size

    def first_stage(i, names, at, count, other, send_sem, recv_sem):
        for h in range(parts[i]):
            rows = pl.ds(*cut(i, h, other))
            spread(
                names, at, 0, count, lambda to: leaving[i].at[to, rows],
                middle[i].at[at, rows], send_sem.at[i], recv_sem.at[i, h],
            )

    def second_stage(i, names, at, count, waited, send_sem, recv_sem):
        for h in range(parts[i]):
            low, size = cut(i, h, count)
            settle(middle[i].at[:, pl.ds(low, size)], waited.at[i, h])
            spread(
                names, at, low, size, lambda to: middle[i].at[:, to],
                landed[i].at[at], send_sem.at[i], recv_sem.at[i, 0],
            )

    leaving = (out_up, out_raw, out_act, done_through, done_across)
    middle = (mid_up, mid_raw, mid_act, mid_through, mid_across)
    landed = (got_up, got_raw, got_act, through_ref, across_ref)
    def leave(i):
        first_stage(i, plane, flat_at, flat, deep, flat_send, flat_recv)

    def pass_on(i):
        second_stage(i, ring, deep_at, deep, flat_recv, deep_send, deep_recv)

    leave(0)
    leave(1)
    pass_on(0)
    leave(2)
    first_chan = (flat_at * deep + deep_at) * chan
    at = at_ref[...]
    for c in range(chan):
        rate = jnp.full((1, cell), rate_ref[first_chan + c], jnp.float32)
        env_ref[:, c * cell : (c + 1) * cell] = jnp.sqrt(2.0 * rate / tokens) * jnp.exp(
            -(rate * at) / tokens
        )
    pass_on(1)
    pass_on(2)
    for copy in held:
        copy.wait()

    inner = (inner_hi_ref[...], inner_lo_ref[...])
    outer = (outer_hi_ref[...], outer_lo_ref[...])

    def arrived(i):
        settle(landed[i], deep_recv.at[i, 0])
        return landed[i][...].reshape(blocks, width)

    def tables(s):
        rows = pl.ds(pl.multiple_of(s * 2 * chunk, 2 * chunk), 2 * chunk)
        few = pl.ds(pl.multiple_of(s * chunk, chunk), chunk)
        return fwd_hi_ref[rows, :], fwd_lo_ref[rows, :], cos_ref[few, :], sin_ref[few, :]

    def forward(values, cosine, sine):
        rows = []
        for c in range(chan):
            re = values[:chunk, c * cell : (c + 1) * cell]
            im = values[chunk:, c * cell : (c + 1) * cell]
            rows.append(
                jnp.concatenate([re * cosine + im * sine, im * cosine - re * sine], axis=1)
            )
        return mul3(halves(jnp.concatenate(rows, axis=0)), inner)

    def inverse(s, other, fwd_hi, fwd_lo, cosine, sine):
        ahead = spec_ref[s]
        up_re, up_im = ahead[:, :cell], ahead[:, cell:]
        re, im = other[:, :cell], other[:, cell:]
        mixed = jnp.concatenate([up_re * re + up_im * im, up_im * re - up_re * im], axis=1)
        back = mul3(halves(mixed), outer)
        parts_re, parts_im = [], []
        for c in range(chan):
            zre = back[c * chunk : (c + 1) * chunk, :cell]
            zim = back[c * chunk : (c + 1) * chunk, cell:]
            parts_re.append(zre * cosine - zim * sine)
            parts_im.append(zim * cosine + zre * sine)
        spread_hi, spread_lo = halves(
            jnp.concatenate(
                [jnp.concatenate(parts_re, axis=1), jnp.concatenate(parts_im, axis=1)], axis=0
            )
        )
        total_ref[...] += mul_left(fwd_hi, spread_hi) + (
            mul_left(fwd_hi, spread_lo) + mul_left(fwd_lo, spread_hi)
        )

    taps_hi_ref[...] = arrived(0)

    def up_step(s, carry):
        fwd_hi, fwd_lo, cosine, sine = tables(s)
        up = taps_hi_ref[...]
        spec_ref[s] = forward(mul(fwd_hi, up) + mul(fwd_lo, up), cosine, sine)
        return carry

    lax.fori_loop(0, steps, up_step, 0)

    taps_hi, taps_lo = halves(arrived(1).astype(jnp.float32) * env_ref[...])
    taps_hi_ref[...] = taps_hi
    taps_lo_ref[...] = taps_lo
    total_ref[...] = jnp.zeros_like(total_ref)

    def taps_step(s, carry):
        fwd_hi, fwd_lo, cosine, sine = tables(s)
        high = taps_hi_ref[...]
        first = mul(fwd_hi, high) + (mul(fwd_hi, taps_lo_ref[...]) + mul(fwd_lo, high))
        inverse(s, forward(first, cosine, sine), fwd_hi, fwd_lo, cosine, sine)
        return carry

    lax.fori_loop(0, steps, taps_step, 0)
    scale = 1.0 / tokens
    up_float = got_up[...].reshape(blocks, width).astype(jnp.float32)
    gain = jnp.concatenate(
        [jnp.full((1, cell), gain_ref[first_chan + c], jnp.float32) for c in range(chan)], axis=1
    )
    through = (total_ref[...] * scale + gain * up_float).astype(jnp.bfloat16)
    done_through[...] = through.reshape(done_through.shape)
    first_stage(3, ring, deep_at, deep, flat, deep_send, deep_recv)

    taps_hi_ref[...] = arrived(2)
    total_ref[...] = jnp.zeros_like(total_ref)

    def act_step(s, carry):
        fwd_hi, fwd_lo, cosine, sine = tables(s)
        act = taps_hi_ref[...]
        first = mul(fwd_hi, act) + mul(fwd_lo, act)
        inverse(s, forward(first, cosine, sine), fwd_hi, fwd_lo, cosine, sine)
        return carry

    lax.fori_loop(0, steps, act_step, 0)
    across = (total_ref[...] * scale * env_ref[...]).astype(jnp.bfloat16)
    done_across[...] = across.reshape(done_across.shape)
    first_stage(4, ring, deep_at, deep, flat, deep_send, deep_recv)
    for i in (3, 4):
        second_stage(i, plane, flat_at, flat, deep_recv, flat_send, flat_recv)
    for i in range(5):
        first_send, last_send = (flat_send, deep_send) if i < 3 else (deep_send, flat_send)
        settle(leaving[i].at[pl.ds(0, leaving[i].shape[0] - 1)], first_send.at[i])
        settle(landed[i].at[pl.ds(0, landed[i].shape[0] - 1)], last_send.at[i])
    for i in (3, 4):
        settle(landed[i], flat_recv.at[i, 0])


def fused(given, decay_rate, skip_gain, places, flat, deep, sizes, interpret):
    cell = given[0].shape[0]
    chan = given[0].shape[1] // (flat * deep)
    blocks, width = flat * deep, chan * cell
    chunk = min(128, blocks)
    steps = blocks // chunk
    length = 2 * blocks * cell
    odd = 2 * np.arange(blocks) + 1
    turns = 2.0 * math.pi * (odd[:, None] * places[None, :] % (4 * blocks)) / (4 * blocks)
    turns = turns.reshape(steps, 1, chunk, blocks)
    fwd = np.concatenate([np.cos(turns), -np.sin(turns)], 1).reshape(2 * blocks, blocks)
    fwd_hi, fwd_lo = table(fwd)
    cells = np.arange(cell)
    turns = 2.0 * math.pi * (cells[:, None] * cells[None, :] % cell) / cell
    inner = np.block([[np.cos(turns), -np.sin(turns)], [np.sin(turns), np.cos(turns)]])
    inner_hi, inner_lo = table(inner)
    outer_hi, outer_lo = table(inner.T)
    turns = 2.0 * math.pi * (odd[:, None] * cells[None, :]) / (2 * length)
    at = (places[:, None] * cell + cells[None, :]).astype(np.float32)
    near = pltpu.VMEM((flat, deep, chan, cell), jnp.bfloat16)
    far = pltpu.VMEM((deep, flat, chan, cell), jnp.bfloat16)
    vmem = pl.BlockSpec(memory_space=pltpu.VMEM)
    smem = pl.BlockSpec(memory_space=pltpu.SMEM)
    return pl.pallas_call(
        functools.partial(fused_kernel, sizes, chunk),
        out_shape=[jax.ShapeDtypeStruct((flat, deep, chan, cell), jnp.bfloat16)] * 2,
        in_specs=[vmem] * 3 + [smem] * 2 + [vmem] + [pl.BlockSpec(memory_space=pl.ANY)] * 2 + [vmem] * 6,
        out_specs=[vmem] * 2,
        scratch_shapes=[near] * 6
        + [far] * 7
        + [
            pltpu.VMEM((steps, chan * chunk, 2 * cell), jnp.float32),
            pltpu.VMEM((blocks, width), jnp.float32),
            pltpu.VMEM((blocks, width), jnp.float32),
            pltpu.VMEM((blocks, width), jnp.bfloat16),
            pltpu.VMEM((blocks, width), jnp.bfloat16),
            pltpu.VMEM((2 * blocks, blocks), jnp.bfloat16),
            pltpu.VMEM((2 * blocks, blocks), jnp.bfloat16),
        ]
        + [pltpu.SemaphoreType.DMA((5,)), pltpu.SemaphoreType.DMA((5, max(4, sizes["zl"])))] * 2
        + [pltpu.SemaphoreType.DMA((2,))],
        compiler_params=pltpu.CompilerParams(collective_id=0, has_side_effects=True),
        interpret=interpret,
    )(
        *given, decay_rate, skip_gain, at, fwd_hi, fwd_lo, inner_hi, inner_lo, outer_hi,
        outer_lo, np.cos(turns).astype(np.float32), np.sin(turns).astype(np.float32),
    )


def per_device(sizes, activation, filter_raw, decay_rate, skip_gain, grad_out, interpret=False):
    cell, model_width = activation.shape
    flat = math.prod(sizes[n] for n in plane)
    deep = math.prod(sizes[n] for n in ring)
    blocks = flat * deep
    row = np.arange(blocks)
    at = {}
    for name in reversed(ring + plane):
        at[name] = row % sizes[name]
        row = row // sizes[name]
    places = 0
    for name in tokens_over:
        places = places * sizes[name] + at[name]
    back = fused(
        (grad_out, filter_raw, activation), decay_rate, skip_gain, places, flat, deep, sizes,
        interpret and pltpu.InterpretParams(),
    )
    return tuple(jnp.transpose(v.reshape(model_width, cell)) for v in back)


def solution(mesh, interpret=False):
    side = round(mesh.shape["seq"] ** (1 / 3))
    chips = mesh.devices.reshape(side, side, side, mesh.shape["sub"] // 2, 2)
    fine = jax.sharding.Mesh(chips, ("x", "zh", "y", "zl", "core"))
    split = P(tokens_over, None)
    return jax.shard_map(
        functools.partial(per_device, dict(fine.shape), interpret=interpret),
        mesh=fine,
        in_specs=(split, split, P(), P(), split),
        out_specs=(split, split),
        check_vma=False,
    )
```

```python
import functools
import math

import jax
import jax.numpy as jnp
import numpy as np
from jax import lax
from jax.experimental import pallas as pl
from jax.experimental.pallas import tpu as pltpu
from jax.sharding import PartitionSpec as P

tokens_over = ("zl", "core", "x", "zh", "y")
plane = ("core", "x", "y")
ring = ("zl", "zh")


def table(values):
    high = values.astype(jnp.bfloat16)
    low = (values - high.astype(np.float64)).astype(jnp.bfloat16)
    return high, low


def halves(values):
    high = values.astype(jnp.bfloat16)
    return high, (values - high.astype(jnp.float32)).astype(jnp.bfloat16)


def mul(left, right):
    return jnp.dot(left, right, preferred_element_type=jnp.float32)


def mul_left(left, right):
    dims = (((0,), (0,)), ((), ()))
    return lax.dot_general(left, right, dims, preferred_element_type=jnp.float32)


def mul3(left, right):
    left_hi, left_lo = left
    right_hi, right_lo = right
    return mul(left_hi, right_hi) + (mul(left_hi, right_lo) + mul(left_lo, right_hi))


def place_of(names, sizes):
    at = 0
    for name in names:
        at = at * sizes[name] + lax.axis_index(name)
    return at


def device_at(names, sizes, at):
    where = {}
    for name in reversed(names):
        where[name] = lax.rem(at, sizes[name])
        at = lax.div(at, sizes[name])
    return where


def fused_kernel(
    sizes, chunk,
    up_ref, raw_ref, act_ref, rate_ref, gain_ref, at_ref, fwd_hi_far, fwd_lo_far,
    inner_hi_ref, inner_lo_ref, outer_hi_ref, outer_lo_ref, cos_ref, sin_ref,
    through_ref, across_ref,
    out_up, out_raw, out_act, mid_up, mid_raw, mid_act, got_up, got_raw, got_act, done_through, done_across,
    mid_through, mid_across, spec_ref, total_ref, env_ref, taps_hi_ref, taps_lo_ref,
    fwd_hi_ref, fwd_lo_ref, early, flat_send, flat_recv, deep_send, deep_recv, held_sem,
):
    flat, deep, chan, cell = out_up.shape
    blocks, width = flat * deep, chan * cell
    steps = blocks // chunk
    tokens = blocks * cell
    flat_at, deep_at = place_of(plane, sizes), place_of(ring, sizes)
    barrier = pltpu.get_barrier_semaphore()
    mesh_id = pl.DeviceIdType.MESH

    def greet(names, at, count):
        def one(k, carry):
            peer = device_at(names, sizes, lax.rem(at + k, count))
            pl.semaphore_signal(barrier, inc=1, device_id=peer, device_id_type=mesh_id)
            return carry

        lax.fori_loop(1, count, one, 0)

    greet(plane, flat_at, flat)
    greet(ring, deep_at, deep)
    held = [
        pltpu.make_async_copy(fwd_hi_far, fwd_hi_ref, held_sem.at[0]),
        pltpu.make_async_copy(fwd_lo_far, fwd_lo_ref, held_sem.at[1]),
    ]
    for copy in held:
        copy.start()
    for given, turned in ((up_ref, out_up), (raw_ref, out_raw), (act_ref, out_act)):
        turned[...] = jnp.transpose(given[...]).reshape(turned.shape)
    pl.semaphore_wait(barrier, flat + deep - 2)

    halves_x = 2 - sizes["x"] % 2
    parts = (sizes["zl"], 1, 1, 1, 2 * halves_x)
    half_at = lax.div(lax.axis_index("x"), sizes["x"] // halves_x)

    def spread(names, at, low, count, piece, landing, send_sem, recv_sem):
        def one(k, carry):
            to = low + lax.rem(at + k, count)

            @pl.when(to != at)
            def _():
                pltpu.make_async_remote_copy(
                    src_ref=piece(to),
                    dst_ref=landing,
                    send_sem=send_sem,
                    recv_sem=recv_sem,
                    device_id=device_at(names, sizes, to),
                    device_id_type=mesh_id,
                ).start()

            @pl.when(to == at)
            def _():
                pltpu.make_async_copy(piece(at), landing, recv_sem).start()

            return carry

        lax.fori_loop(1, count + 1, one, 0)

    def settle(ref, sem):
        pltpu.make_async_copy(ref, ref, sem).wait()

    def cut(i, h, count):
        size = count // parts[i]
        slot = 0
        if i == 0:
            slot = lax.rem(lax.axis_index("zl") + h, sizes["zl"])
        if i == 4:
            core = lax.rem(lax.axis_index("core") + 1 - h // halves_x, 2)
            half = lax.rem(half_at + halves_x - 1 - h % halves_x, halves_x)
            slot = core * halves_x + half
        return slot * size, size

    def first_stage(i, names, at, count, other, send_sem, recv_sem):
        for h in range(parts[i]):
            rows = pl.ds(*cut(i, h, other))
            spread(
                names, at, 0, count, lambda to: leaving[i].at[to, rows],
                middle[i].at[at, rows], send_sem.at[i], recv_sem.at[i, h],
            )

    def second_stage(i, names, at, count, waited, send_sem, recv_sem):
        for h in range(parts[i]):
            low, size = cut(i, h, count)
            settle(middle[i].at[:, pl.ds(low, size)], waited.at[i, h])
            spread(
                names, at, low, size, lambda to: middle[i].at[:, to],
                landed[i].at[at], send_sem.at[i], recv_sem.at[i, 0],
            )

    leaving = (out_up, out_raw, out_act, done_through, done_across)
    middle = (mid_up, mid_raw, mid_act, mid_through, mid_across)
    landed = (got_up, got_raw, got_act, through_ref, across_ref)
    def leave(i):
        first_stage(i, plane, flat_at, flat, deep, flat_send, flat_recv)

    def pass_on(i):
        second_stage(i, ring, deep_at, deep, flat_recv, deep_send, deep_recv)

    groups, size = sizes["zl"], sizes["zh"]
    zl_at, zh_at = lax.axis_index("zl"), lax.axis_index("zh")
    spread(
        ring, deep_at, zl_at * size, size, lambda to: out_act.at[:, to],
        early.at[zh_at], deep_send.at[2], deep_recv.at[2, 1],
    )
    leave(0)
    leave(1)
    pass_on(0)
    for h in range(1, groups):
        rows = pl.ds(lax.rem(zl_at + h, groups) * size, size)
        spread(
            plane, flat_at, 0, flat, lambda to: out_act.at[to, rows],
            mid_act.at[flat_at, rows], flat_send.at[2], flat_recv.at[2, h - 1],
        )
    first_chan = (flat_at * deep + deep_at) * chan
    at = at_ref[...]
    for c in range(chan):
        rate = jnp.full((1, cell), rate_ref[first_chan + c], jnp.float32)
        env_ref[:, c * cell : (c + 1) * cell] = jnp.sqrt(2.0 * rate / tokens) * jnp.exp(
            -(rate * at) / tokens
        )
    pass_on(1)
    for h in range(1, groups):
        low = lax.rem(zl_at + h, groups) * size
        settle(mid_act.at[:, pl.ds(low, size)], flat_recv.at[2, h - 1])
        spread(
            ring, deep_at, low, size, lambda to: mid_act.at[:, to],
            got_act.at[deep_at], deep_send.at[2], deep_recv.at[2, 0],
        )
    own_rows = pl.ds(zl_at * size, size)
    settle(early, deep_recv.at[2, 1])
    spread(
        plane, flat_at, 0, flat, lambda to: early.at[:, to],
        got_act.at[own_rows, flat_at], flat_send.at[2], flat_recv.at[2, groups - 1],
    )
    for copy in held:
        copy.wait()

    inner = (inner_hi_ref[...], inner_lo_ref[...])
    outer = (outer_hi_ref[...], outer_lo_ref[...])

    def arrived(i):
        if i < 2:
            settle(landed[i], deep_recv.at[i, 0])
        else:
            if groups > 1:
                settle(got_act.at[pl.ds(0, deep - size)], deep_recv.at[2, 0])
            settle(got_act.at[own_rows], flat_recv.at[2, groups - 1])
        return landed[i][...].reshape(blocks, width)

    def tables(s):
        rows = pl.ds(pl.multiple_of(s * 2 * chunk, 2 * chunk), 2 * chunk)
        few = pl.ds(pl.multiple_of(s * chunk, chunk), chunk)
        return fwd_hi_ref[rows, :], fwd_lo_ref[rows, :], cos_ref[few, :], sin_ref[few, :]

    def forward(values, cosine, sine):
        rows = []
        for c in range(chan):
            re = values[:chunk, c * cell : (c + 1) * cell]
            im = values[chunk:, c * cell : (c + 1) * cell]
            rows.append(
                jnp.concatenate([re * cosine + im * sine, im * cosine - re * sine], axis=1)
            )
        return mul3(halves(jnp.concatenate(rows, axis=0)), inner)

    def inverse(s, other, fwd_hi, fwd_lo, cosine, sine):
        ahead = spec_ref[s]
        up_re, up_im = ahead[:, :cell], ahead[:, cell:]
        re, im = other[:, :cell], other[:, cell:]
        mixed = jnp.concatenate([up_re * re + up_im * im, up_im * re - up_re * im], axis=1)
        back = mul3(halves(mixed), outer)
        parts_re, parts_im = [], []
        for c in range(chan):
            zre = back[c * chunk : (c + 1) * chunk, :cell]
            zim = back[c * chunk : (c + 1) * chunk, cell:]
            parts_re.append(zre * cosine - zim * sine)
            parts_im.append(zim * cosine + zre * sine)
        spread_hi, spread_lo = halves(
            jnp.concatenate(
                [jnp.concatenate(parts_re, axis=1), jnp.concatenate(parts_im, axis=1)], axis=0
            )
        )
        total_ref[...] += mul_left(fwd_hi, spread_hi) + (
            mul_left(fwd_hi, spread_lo) + mul_left(fwd_lo, spread_hi)
        )

    taps_hi_ref[...] = arrived(0)

    def up_step(s, carry):
        fwd_hi, fwd_lo, cosine, sine = tables(s)
        up = taps_hi_ref[...]
        spec_ref[s] = forward(mul(fwd_hi, up) + mul(fwd_lo, up), cosine, sine)
        return carry

    lax.fori_loop(0, steps, up_step, 0)

    taps_hi, taps_lo = halves(arrived(1).astype(jnp.float32) * env_ref[...])
    taps_hi_ref[...] = taps_hi
    taps_lo_ref[...] = taps_lo
    total_ref[...] = jnp.zeros_like(total_ref)

    def taps_step(s, carry):
        fwd_hi, fwd_lo, cosine, sine = tables(s)
        high = taps_hi_ref[...]
        first = mul(fwd_hi, high) + (mul(fwd_hi, taps_lo_ref[...]) + mul(fwd_lo, high))
        inverse(s, forward(first, cosine, sine), fwd_hi, fwd_lo, cosine, sine)
        return carry

    lax.fori_loop(0, steps, taps_step, 0)
    scale = 1.0 / tokens
    up_float = got_up[...].reshape(blocks, width).astype(jnp.float32)
    gain = jnp.concatenate(
        [jnp.full((1, cell), gain_ref[first_chan + c], jnp.float32) for c in range(chan)], axis=1
    )
    through = (total_ref[...] * scale + gain * up_float).astype(jnp.bfloat16)
    done_through[...] = through.reshape(done_through.shape)
    first_stage(3, ring, deep_at, deep, flat, deep_send, deep_recv)

    taps_hi_ref[...] = arrived(2)
    total_ref[...] = jnp.zeros_like(total_ref)

    def act_step(s, carry):
        fwd_hi, fwd_lo, cosine, sine = tables(s)
        act = taps_hi_ref[...]
        first = mul(fwd_hi, act) + mul(fwd_lo, act)
        inverse(s, forward(first, cosine, sine), fwd_hi, fwd_lo, cosine, sine)
        return carry

    lax.fori_loop(0, steps, act_step, 0)
    across = (total_ref[...] * scale * env_ref[...]).astype(jnp.bfloat16)
    done_across[...] = across.reshape(done_across.shape)
    first_stage(4, ring, deep_at, deep, flat, deep_send, deep_recv)
    for i in (3, 4):
        second_stage(i, plane, flat_at, flat, deep_recv, flat_send, flat_recv)
    for i in range(5):
        first_send, last_send = (flat_send, deep_send) if i < 3 else (deep_send, flat_send)
        settle(leaving[i].at[pl.ds(0, leaving[i].shape[0] - 1)], first_send.at[i])
        settle(landed[i].at[pl.ds(0, landed[i].shape[0] - 1)], last_send.at[i])
    for i in (3, 4):
        settle(landed[i], flat_recv.at[i, 0])


def fused(given, decay_rate, skip_gain, places, flat, deep, sizes, interpret):
    cell = given[0].shape[0]
    chan = given[0].shape[1] // (flat * deep)
    blocks, width = flat * deep, chan * cell
    chunk = min(128, blocks)
    steps = blocks // chunk
    length = 2 * blocks * cell
    odd = 2 * np.arange(blocks) + 1
    turns = 2.0 * math.pi * (odd[:, None] * places[None, :] % (4 * blocks)) / (4 * blocks)
    turns = turns.reshape(steps, 1, chunk, blocks)
    fwd = np.concatenate([np.cos(turns), -np.sin(turns)], 1).reshape(2 * blocks, blocks)
    fwd_hi, fwd_lo = table(fwd)
    cells = np.arange(cell)
    turns = 2.0 * math.pi * (cells[:, None] * cells[None, :] % cell) / cell
    inner = np.block([[np.cos(turns), -np.sin(turns)], [np.sin(turns), np.cos(turns)]])
    inner_hi, inner_lo = table(inner)
    outer_hi, outer_lo = table(inner.T)
    turns = 2.0 * math.pi * (odd[:, None] * cells[None, :]) / (2 * length)
    at = (places[:, None] * cell + cells[None, :]).astype(np.float32)
    near = pltpu.VMEM((flat, deep, chan, cell), jnp.bfloat16)
    far = pltpu.VMEM((deep, flat, chan, cell), jnp.bfloat16)
    vmem = pl.BlockSpec(memory_space=pltpu.VMEM)
    smem = pl.BlockSpec(memory_space=pltpu.SMEM)
    return pl.pallas_call(
        functools.partial(fused_kernel, sizes, chunk),
        out_shape=[jax.ShapeDtypeStruct((flat, deep, chan, cell), jnp.bfloat16)] * 2,
        in_specs=[vmem] * 3 + [smem] * 2 + [vmem] + [pl.BlockSpec(memory_space=pl.ANY)] * 2 + [vmem] * 6,
        out_specs=[vmem] * 2,
        scratch_shapes=[near] * 6
        + [far] * 7
        + [
            pltpu.VMEM((steps, chan * chunk, 2 * cell), jnp.float32),
            pltpu.VMEM((blocks, width), jnp.float32),
            pltpu.VMEM((blocks, width), jnp.float32),
            pltpu.VMEM((blocks, width), jnp.bfloat16),
            pltpu.VMEM((blocks, width), jnp.bfloat16),
            pltpu.VMEM((2 * blocks, blocks), jnp.bfloat16),
            pltpu.VMEM((2 * blocks, blocks), jnp.bfloat16),
            pltpu.VMEM((sizes["zh"], flat, chan, cell), jnp.bfloat16),
        ]
        + [pltpu.SemaphoreType.DMA((5,)), pltpu.SemaphoreType.DMA((5, max(4, sizes["zl"])))] * 2
        + [pltpu.SemaphoreType.DMA((2,))],
        compiler_params=pltpu.CompilerParams(collective_id=0, has_side_effects=True),
        interpret=interpret,
    )(
        *given, decay_rate, skip_gain, at, fwd_hi, fwd_lo, inner_hi, inner_lo, outer_hi,
        outer_lo, np.cos(turns).astype(np.float32), np.sin(turns).astype(np.float32),
    )


def per_device(sizes, activation, filter_raw, decay_rate, skip_gain, grad_out, interpret=False):
    cell, model_width = activation.shape
    flat = math.prod(sizes[n] for n in plane)
    deep = math.prod(sizes[n] for n in ring)
    blocks = flat * deep
    row = np.arange(blocks)
    at = {}
    for name in reversed(ring + plane):
        at[name] = row % sizes[name]
        row = row // sizes[name]
    places = 0
    for name in tokens_over:
        places = places * sizes[name] + at[name]
    back = fused(
        (grad_out, filter_raw, activation), decay_rate, skip_gain, places, flat, deep, sizes,
        interpret and pltpu.InterpretParams(),
    )
    return tuple(jnp.transpose(v.reshape(model_width, cell)) for v in back)


def solution(mesh, interpret=False):
    side = round(mesh.shape["seq"] ** (1 / 3))
    chips = mesh.devices.reshape(side, side, side, mesh.shape["sub"] // 2, 2)
    fine = jax.sharding.Mesh(chips, ("x", "zh", "y", "zl", "core"))
    split = P(tokens_over, None)
    return jax.shard_map(
        functools.partial(per_device, dict(fine.shape), interpret=interpret),
        mesh=fine,
        in_specs=(split, split, P(), P(), split),
        out_specs=(split, split),
        check_vma=False,
    )
```
